256 devices in a mesh: group: 32 (over y_hi, z, core), tok: 8 (over x, y_lo).
Axes of the slice: x: 4, y: 4 (y_hi: 2, y_lo: 2; y = y_hi * 2 + y_lo), z: 8, core: 2. Of those that a mesh axis runs over, the one named last changes fastest.
Arguments:
- latents: bfloat16 [32768, 5120], P(('group', 'tok')), may hold values from -6 to 6
- timesteps: int32 [32], P('group'), may hold values from 0 to 999
- mod_shift: float32 [5120], replicated, may hold values from -3 to 3
- mod_scale: float32 [5120], replicated, may hold values from -1.5 to 1.5
- w_query: bfloat16 [5120, 3072], P('group', 'tok'), may hold values from -7 to 7
- w_key: bfloat16 [5120, 3072], P('group', 'tok'), may hold values from -7 to 7
- w_value: bfloat16 [5120, 3072], P('group', 'tok'), may hold values from -0.078125 to 0.078125
- query_gain: float32 [3072], P('tok'), may hold values from 0.5 to 1.5
- key_gain: float32 [3072], P('tok'), may hold values from 0.5 to 1.5
- cache_keys: bfloat16 [32768, 3072], P('group', 'tok'), may hold values from -85 to 85
- cache_values: bfloat16 [32768, 3072], P('group', 'tok'), may hold values from -6 to 6
- owners: int32 [32], replicated, may hold values from 0 to 31, each once
- tile_mask: int32 [24, 8, 24], P('tok'), may hold values from 0 to 1, as said below
Outputs:
- attended: bfloat16 [32768, 3072], P('group', 'tok')
The draws below stay inside these ranges and needn't reach their ends.
Inputs may be any that keep to these rules, and one draw needn't show every extreme that they name: `tile_mask`: each query tile i of each head sees 1 to 8 key tiles, always tile 2 * 8 + i; some query tile sees exactly 8.
All inputs are finite; a program needn't handle non-finite values.
Results may differ from the reference program's by a relative error of at most 0.012.
The reference program's roundings to bfloat16 on the way count: a program that leaves them out, or rounds other values in their place, can miss the bound.
Values may be sent and summed in bfloat16 or wider, within the bound.
No kernel may reach another device: no remote copies, remote signals or barrier semaphores. Data moves between devices by JAX's collectives and lax.ppermute only.
A program may use at most 128 MiB of HBM per device.

```python
import math
import jax
import jax.numpy as jnp
from jax import lax

D = 5120
HEADS = 24
HEAD_DIM = 128
TILE = 128
GROUP_ROWS = 1024
N_GROUP_ROWS_ALL = 32768
QTILES = 8
KTILES = 24
MOST = 8
N_GROUP = 32


def rising_weight(key, salt):
    base = jnp.clip(jax.random.normal(jax.random.fold_in(key, salt), (D, HEADS * HEAD_DIM), jnp.float32), -6.0, 6.0)
    head_index = (jnp.arange(HEADS * HEAD_DIM) // HEAD_DIM).astype(jnp.float32)
    rising = jnp.exp(math.log(3.0) * head_index / max(HEADS - 1, 1))
    return (base * rising * D ** (-0.5)).astype(jnp.bfloat16)


def draw_w_query(key, part):
    return rising_weight(key, 11)


def draw_w_key(key, part):
    return rising_weight(key, 23)


def draw_cache_keys(key, part):
    shape = (N_GROUP * GROUP_ROWS, HEADS * HEAD_DIM)
    first_key = jax.random.fold_in(key, 31)
    values = jnp.clip(jax.random.normal(first_key, shape, jnp.float32), -4.0, 4.0)
    return values.astype(jnp.bfloat16)


def draw_tile_mask(key, part):
    base_key = jax.random.fold_in(key, 51)
    jitter_key = jax.random.fold_in(key, 52)
    spot_key = jax.random.fold_in(key, 53)
    order_key = jax.random.fold_in(key, 54)
    base_count = jax.random.randint(base_key, (HEADS, 1), 1, MOST - 1)
    jitter = jax.random.randint(jitter_key, (HEADS, QTILES), 0, 3)
    counts = jnp.minimum(base_count + jitter, MOST)
    spot = jax.random.randint(spot_key, (), 0, HEADS * QTILES)
    flat_index = jnp.arange(HEADS * QTILES).reshape(HEADS, QTILES)
    counts = jnp.where(flat_index == spot, MOST, counts)
    priority = jax.random.randint(order_key, (HEADS, QTILES, KTILES), 0, 1 << 20) * KTILES + jnp.arange(KTILES)[None, None, :]
    diagonal = jnp.arange(KTILES)[None, None, :] == (2 * QTILES + jnp.arange(QTILES))[None, :, None]
    priority = jnp.where(diagonal, 1 << 30, priority)
    ranks = jnp.argsort(jnp.argsort(-priority, axis=-1, stable=True), axis=-1, stable=True)
    return (ranks < counts[:, :, None]).astype(jnp.int32)


def plant(array, key, least, largest):
    longest = array.shape.index(max(array.shape))
    spots = []
    for shift in (0, 1):
        where = [jax.random.randint(jax.random.fold_in(key, axis), (), 0, length) for axis, length in enumerate(array.shape)]
        where[longest] = (where[longest] + shift) % array.shape[longest]
        spots.append(tuple(where))
    return array.at[spots[0]].set(least).at[spots[1]].set(largest)


def levels(stream_key, dims, split, smallest, high):
    def one(axis_at, parts):
        draws = jax.random.uniform(jax.random.fold_in(jax.random.fold_in(stream_key, 6), axis_at), (parts,), jnp.float32, smallest / len(split), high / len(split))
        return jnp.repeat(jnp.exp(draws), dims[axis_at] // parts).reshape((-1,) + (1,) * (len(dims) - axis_at - 1))

    factor_of = one(*split[0])
    for cut in split[1:]:
        factor_of = factor_of * one(*cut)
    return factor_of


def noise(key, dims, scale, most, shards=(), held_as=jnp.bfloat16):
    level = levels(key, dims, shards, -0.22, 0.18) if shards else 1.0
    array = jax.random.normal(key, dims, jnp.float32) * scale * level
    return jnp.minimum(jnp.maximum(array, -most), most).astype(held_as)


def setup_inputs(seed: int = 0) -> dict:
    key_of = jax.random.split(jax.random.key(seed), 14)
    latents = noise(key_of[0], (N_GROUP_ROWS_ALL, D), 1.0, 6.0, ((0, 256),))
    timesteps = plant(jax.random.randint(key_of[1], (N_GROUP,), 0, 1000), jax.random.fold_in(key_of[1], 1), 0, 999).astype(jnp.int32)
    mod_shift = noise(key_of[2], (D,), 0.5, 3.0, (), jnp.float32)
    mod_scale = noise(key_of[3], (D,), 0.3, 1.5, (), jnp.float32)
    w_query = draw_w_query(jax.random.fold_in(key_of[13], 71), 0)
    w_key = draw_w_key(jax.random.fold_in(key_of[13], 71), 0)
    w_value = noise(key_of[6], (D, HEADS * HEAD_DIM), D ** -0.5, 0.078125, ((0, 32), (1, 8)))
    query_gain = jnp.clip(1.0 + 0.1 * jax.random.normal(key_of[7], (HEADS * HEAD_DIM,), jnp.float32), 0.5, 1.5)
    key_gain = jnp.clip(1.0 + 0.1 * jax.random.normal(key_of[8], (HEADS * HEAD_DIM,), jnp.float32), 0.5, 1.5)
    cache_keys = draw_cache_keys(jax.random.fold_in(key_of[13], 71), 0)
    cache_values = noise(key_of[10], (N_GROUP_ROWS_ALL, HEADS * HEAD_DIM), 1.0, 6.0, ((0, 32), (1, 8)))
    owners = jax.random.permutation(key_of[11], N_GROUP).astype(jnp.int32)
    tile_mask = draw_tile_mask(jax.random.fold_in(key_of[13], 71), 0)
    return {"latents": latents, "timesteps": timesteps, "mod_shift": mod_shift, "mod_scale": mod_scale, "w_query": w_query, "w_key": w_key, "w_value": w_value, "query_gain": query_gain, "key_gain": key_gain, "cache_keys": cache_keys, "cache_values": cache_values, "owners": owners, "tile_mask": tile_mask}


EPSILON = 1e-06

def modulate(rows_block, timestep, mod_shift, mod_scale):
    values = rows_block.astype(jnp.float32)
    width = values.shape[-1]
    centred = values - lax.optimization_barrier(jnp.mean(values, axis=-1, keepdims=True))
    spread = lax.optimization_barrier(jnp.mean(centred * centred, axis=-1, keepdims=True))
    normed = centred * lax.rsqrt(spread + EPSILON)
    freqs = jnp.exp(-math.log(10000.0) * jnp.arange(width, dtype=jnp.float32) / width)
    angles = timestep.astype(jnp.float32) * freqs
    return (normed * (1.0 + mod_scale + 0.5 * jnp.cos(angles)) + mod_shift + 0.5 * jnp.sin(angles)).astype(jnp.bfloat16)

def head_normed(raw, gain):
    squares = lax.optimization_barrier(jnp.mean(raw * raw, axis=-1, keepdims=True))
    return (raw * lax.rsqrt(squares + EPSILON) * gain).astype(jnp.bfloat16)

def reference(latents, timesteps, mod_shift, mod_scale, w_query, w_key, w_value, query_gain, key_gain, cache_keys, cache_values, owners, tile_mask):
    width = HEADS * HEAD_DIM
    score_scale = 1.0 / math.sqrt(HEAD_DIM)

    def project(operands):
        rows_block, timestep = operands
        modulated = modulate(rows_block, timestep, mod_shift, mod_scale)
        raw_query = jnp.dot(modulated, w_query, preferred_element_type=jnp.float32)
        raw_key = jnp.dot(modulated, w_key, preferred_element_type=jnp.float32)
        raw_value = jnp.dot(modulated, w_value, preferred_element_type=jnp.float32)
        return (head_normed(raw_query, query_gain), head_normed(raw_key, key_gain), raw_value.astype(jnp.bfloat16))
    groups = latents.reshape(N_GROUP, GROUP_ROWS, D)
    queries, keys_all, values_all = lax.map(project, (groups, timesteps))
    root = owners[N_GROUP - 1].astype(jnp.int32)
    cached_keys = lax.dynamic_slice_in_dim(cache_keys, root * GROUP_ROWS, GROUP_ROWS, 0)
    cached_values = lax.dynamic_slice_in_dim(cache_values, root * GROUP_ROWS, GROUP_ROWS, 0)
    tile_ids = jnp.arange(KTILES, dtype=jnp.int32)
    earlier_region = (tile_ids >= QTILES) & (tile_ids < 2 * QTILES)

    def one_head(operands):
        query_head, key_head, value_head, head_mask = operands
        row_mask = jnp.repeat(jnp.repeat(head_mask, TILE, axis=0), TILE, axis=1)
        scores = jnp.dot(query_head, key_head.T, preferred_element_type=jnp.float32) * score_scale
        scores = jnp.where(row_mask > 0, scores, -jnp.inf)
        peak = lax.optimization_barrier(jnp.max(scores, axis=-1, keepdims=True))
        weights = jnp.exp(scores - peak)
        low_weights = weights.astype(jnp.bfloat16)
        summed = jnp.dot(low_weights, value_head, preferred_element_type=jnp.float32)
        return (summed / lax.optimization_barrier(jnp.sum(weights, axis=-1, keepdims=True))).astype(jnp.bfloat16)

    def attend_group(group_index):
        earlier = jnp.maximum(group_index - 1, 0)
        context_keys = jnp.concatenate([cached_keys, keys_all[earlier], keys_all[group_index]], axis=0)
        context_values = jnp.concatenate([cached_values, values_all[earlier], values_all[group_index]], axis=0)
        allowed = jnp.where(earlier_region[None, None, :] & (group_index == 0), 0, tile_mask)
        query_heads = queries[group_index].reshape(GROUP_ROWS, HEADS, HEAD_DIM).transpose(1, 0, 2)
        key_heads = context_keys.reshape(3 * GROUP_ROWS, HEADS, HEAD_DIM).transpose(1, 0, 2)
        value_heads = context_values.reshape(3 * GROUP_ROWS, HEADS, HEAD_DIM).transpose(1, 0, 2)
        attended = lax.map(one_head, (query_heads, key_heads, value_heads, allowed))
        return attended.transpose(1, 0, 2).reshape(GROUP_ROWS, width)
    outputs = lax.map(attend_group, jnp.arange(N_GROUP, dtype=jnp.int32))
    return outputs.reshape(N_GROUP * GROUP_ROWS, width)
```

```python
import functools
import math

import jax
import jax.numpy as jnp
from jax import lax
from jax.experimental import pallas as pl
from jax.experimental.pallas import tpu as pltpu
from jax.sharding import PartitionSpec as P

EPSILON = 1e-06
TILE = 128
MOST = 8
FAR = -1e30
NY, NZ, NC, NX = 2, 8, 2, 4
SLOT_OF = (0, 1, 3, 5, 6, 7, 2, 4)
INTERPRET = False


def group_shift(value, dz=0, dc=0, dy=0):
    def at(y, z, c):
        return (y % NY) * NZ * NC + (z % NZ) * NC + c % NC

    route = [
        (at(y, z, c), at(y + dy, z + dz, c + dc))
        for y in range(NY)
        for z in range(NZ)
        for c in range(NC)
    ]
    return lax.ppermute(value, "group", route)


def tok_shift(value, dx=0, dy=0):
    route = [
        (x * 2 + y, ((x + dx) % NX) * 2 + (y + dy) % 2) for x in range(NX) for y in range(2)
    ]
    return lax.ppermute(value, "tok", route)


def from_behind(block, axis, distance):
    devices = range(lax.axis_size(axis))
    route = [(i - distance, i) for i in devices if i - distance in devices]
    return lax.ppermute(block, axis, route)


def modulate(rows_block, timestep, mod_shift, mod_scale):
    values = rows_block.astype(jnp.float32)
    width = values.shape[-1]
    centred = values - jnp.mean(values, axis=-1, keepdims=True)
    spread = jnp.mean(centred * centred, axis=-1, keepdims=True)
    normed = centred * lax.rsqrt(spread + EPSILON)
    freqs = jnp.exp(-math.log(10000.0) * jnp.arange(width, dtype=jnp.float32) / width)
    angles = timestep.astype(jnp.float32) * freqs
    return (
        normed * (1.0 + mod_scale + 0.5 * jnp.cos(angles)) + mod_shift + 0.5 * jnp.sin(angles)
    ).astype(jnp.bfloat16)


def scaled_rows(raw, squares, width, gain):
    return (raw * lax.rsqrt(squares / width + EPSILON)[:, None] * gain).astype(jnp.bfloat16)


def gather_tokens(own):
    half = own.shape[0] // 2
    beside = tok_shift(own, 0, 1)
    own_lo = tok_shift(own, 1)
    own_hi = tok_shift(own, -1)
    far_a = tok_shift(own_lo[:half], 1)
    far_b = tok_shift(own_hi[half:], -1)
    side_lo = tok_shift(beside, 1)
    side_hi = tok_shift(beside, -1)
    far_c = tok_shift(side_lo[:half], 1)
    far_d = tok_shift(side_hi[half:], -1)
    return (own, beside, own_lo, own_hi, side_lo, side_hi, far_a, far_b, far_c, far_d)


def tok_shift_rows(value, dx=0, dy=0):
    came = tok_shift(value, dx, dy).reshape(2 * NX, -1)
    picks = [0] * (2 * NX)
    for n, slot in enumerate(SLOT_OF):
        picks[slot] = SLOT_OF[((n // 2 + dx) % NX) * 2 + (n % 2 + dy) % 2]
    return jnp.concatenate([came[p] for p in picks])


def sum_over_tok(value):
    pair = value + tok_shift_rows(value, 0, 1)
    parts = [tok_shift_rows(pair, k) for k in (1, 3, 2)]
    return (pair + parts[0]) + (parts[1] + parts[2])


def spread_cache(cache_keys, cache_values, root):
    me = lax.axis_index("group")
    root_y, root_z, root_c = root >> 4, (root >> 1) & (NZ - 1), root & 1
    my_y, my_z, my_c = me >> 4, (me >> 1) & (NZ - 1), me & 1
    first = my_c == 0
    mine = jnp.where(first, cache_keys, cache_values)
    other = jnp.where(first, cache_values, cache_keys)
    across = group_shift(other, dc=1)
    held = jnp.where(my_c == root_c, mine, across)
    rows = held.shape[0]
    piece = rows // NZ
    got = jnp.where(my_z == root_z, lax.dynamic_slice_in_dim(held, my_z * piece, piece, 0), 0)
    for k in range(1, NZ):
        target = (my_z + k) & (NZ - 1)
        sent = lax.dynamic_slice_in_dim(held, target * piece, piece, 0)
        came = group_shift(sent, dz=k)
        got = jnp.where((my_z + NZ - k) & (NZ - 1) == root_z, came, got)
    from_y = group_shift(got, dy=1)
    got = jnp.where(my_y == root_y, got, from_y)
    rings = [
        [y * NZ * NC + z * NC + c for z in range(NZ)] for y in range(NY) for c in range(NC)
    ]
    whole = lax.all_gather(got, "group", axis_index_groups=rings, axis=0, tiled=True)
    swapped = group_shift(whole, dc=1)
    return jnp.where(first, whole, swapped), jnp.where(first, swapped, whole)


def project_kernel(count, *refs):
    blocks, weight, out, acc = refs[:count], refs[count], refs[count + 1], refs[count + 2]
    step = pl.program_id(0)

    @pl.when(step == 0)
    def _():
        acc[...] = jnp.zeros_like(acc)

    rows = jnp.concatenate([block[...] for block in blocks], axis=0)
    acc[...] += jnp.dot(rows, weight[...], preferred_element_type=jnp.float32)

    @pl.when(step == pl.num_programs(0) - 1)
    def _():
        out[...] = acc[...]


def project(blocks, weight, start, columns, depth):
    features = weight.shape[0]
    rows = sum(block.shape[0] for block in blocks)
    block_at = start // columns
    return pl.pallas_call(
        functools.partial(project_kernel, len(blocks)),
        grid=(features // depth,),
        in_specs=[pl.BlockSpec((b.shape[0], depth), lambda k: (0, k)) for b in blocks]
        + [pl.BlockSpec((depth, columns), lambda k: (k, block_at))],
        out_specs=pl.BlockSpec((rows, columns), lambda k: (0, 0)),
        out_shape=jax.ShapeDtypeStruct((rows, columns), jnp.float32),
        scratch_shapes=[pltpu.VMEM((rows, columns), jnp.float32)],
        compiler_params=pltpu.CompilerParams(dimension_semantics=("arbitrary",)),
        cost_estimate=pl.CostEstimate(
            flops=2 * rows * columns * features,
            transcendentals=0,
            bytes_accessed=2 * features * (rows + columns) + 4 * rows * columns,
        ),
        interpret=INTERPRET,
        name="project",
    )(*blocks, weight)


def attend_kernel(
    heads, scale, order, count, slots, query, ck, cv, ek, ev, nk, nv, out, keys, values, sems
):
    span = ck.shape[0]
    parts = ((ck, cv), (ek, ev), (nk, nv))
    copies = []
    for n, (k_part, v_part) in enumerate(parts):
        rows = pl.ds(n * span, span)
        copies.append(pltpu.make_async_copy(k_part, keys.at[rows], sems.at[2 * n]))
        copies.append(pltpu.make_async_copy(v_part, values.at[rows], sems.at[2 * n + 1]))
    for copy in copies:
        copy.start()
    for copy in copies:
        copy.wait()
    tiles = span // TILE

    def one_tile(i, pairs):
        from_row = pl.multiple_of(slots[i] * TILE, TILE)
        to_row = pl.multiple_of(i * TILE, TILE)
        low = lax.broadcasted_iota(jnp.int32, (1, 2 * TILE), 1) < TILE
        for h in range(heads):
            cols = pl.ds(h * TILE, TILE)
            at = h * tiles + i
            seen = count[at]
            q = query[pl.ds(from_row, TILE), cols]
            scores, vals = [], []
            for p in range(pairs):
                rows = [
                    pl.ds(pl.multiple_of(order[at * MOST + 2 * p + s] * TILE, TILE), TILE)
                    for s in range(2)
                ]
                k_pair = jnp.concatenate([keys[r, cols] for r in rows], axis=0)
                vals.append(jnp.concatenate([values[r, cols] for r in rows], axis=0))
                s = lax.dot_general(
                    q, k_pair, (((1,), (1,)), ((), ())), preferred_element_type=jnp.float32
                )
                bias = jnp.where(
                    low,
                    jnp.where(2 * p < seen, 0.0, FAR),
                    jnp.where(2 * p + 1 < seen, 0.0, FAR),
                )
                scores.append(s * scale + bias)
            top = scores[0]
            for s in scores[1:]:
                top = jnp.maximum(top, s)
            peak = jnp.max(top, axis=1, keepdims=True)
            total, summed = None, None
            for s, v in zip(scores, vals):
                probs = jnp.exp(s - peak)
                total = probs if total is None else total + probs
                added = jnp.dot(probs.astype(jnp.bfloat16), v, preferred_element_type=jnp.float32)
                summed = added if summed is None else summed + added
            denominator = jnp.sum(total, axis=1, keepdims=True)
            out[pl.ds(to_row, TILE), cols] = (summed / denominator).astype(jnp.bfloat16)

    @pl.loop(0, tiles)
    def _(i):
        most = count[i]
        for h in range(1, heads):
            most = jnp.maximum(most, count[h * tiles + i])
        for pairs in range(1, MOST // 2 + 1):
            pl.when((most + 1) // 2 == pairs)(functools.partial(one_tile, i, pairs))


def attend(query, parts, order, count, slots, heads):
    rows, width = query.shape
    anywhere = pl.BlockSpec(memory_space=pl.ANY)
    whole = pl.BlockSpec(memory_space=pltpu.VMEM)
    return pl.pallas_call(
        functools.partial(attend_kernel, heads, 1.0 / math.sqrt(width // heads)),
        grid_spec=pltpu.PrefetchScalarGridSpec(
            num_scalar_prefetch=3,
            grid=(),
            in_specs=[whole] + [anywhere] * 6,
            out_specs=whole,
            scratch_shapes=[
                pltpu.VMEM((3 * rows, width), jnp.bfloat16),
                pltpu.VMEM((3 * rows, width), jnp.bfloat16),
                pltpu.SemaphoreType.DMA((6,)),
            ],
        ),
        out_shape=jax.ShapeDtypeStruct((rows, width), jnp.bfloat16),
        cost_estimate=pl.CostEstimate(
            flops=4 * rows * width * MOST * TILE,
            transcendentals=rows * heads * MOST * TILE,
            bytes_accessed=16 * rows * width,
        ),
        interpret=INTERPRET,
        name="attend",
    )(order, count, slots, query, *parts)


def tile_lists(tile_mask, is_first, tok):
    tiles, key_tiles = tile_mask.shape[1], tile_mask.shape[2]
    ids = jnp.arange(key_tiles, dtype=jnp.int32)
    earlier = (ids >= tiles) & (ids < 2 * tiles)
    allowed = jnp.where(earlier[None, None, :] & is_first, 0, tile_mask)
    count = jnp.sum(allowed, axis=-1)
    upto = (ids[None, :] <= ids[:, None]).astype(jnp.int32)
    rank = jnp.sum(allowed[:, :, None, :] * upto, axis=-1)
    places = jnp.arange(tiles, dtype=jnp.int32)
    step = (((places >> 1) - (tok >> 1)) & (NX - 1)) * 2 + ((places ^ tok) & 1)
    slots = sum(jnp.where(step == n, slot, 0) for n, slot in enumerate(SLOT_OF))
    physical = jnp.concatenate([places, tiles + slots, 2 * tiles + slots])
    turn = jnp.arange(1, MOST + 1, dtype=jnp.int32)
    picked = (rank[:, :, None, :] == turn[None, None, :, None]) & (allowed[:, :, None, :] > 0)
    order = jnp.sum(jnp.where(picked, physical, 0), axis=-1)
    return order.reshape(-1), count.reshape(-1), slots


def local(
    latents,
    timesteps,
    mod_shift,
    mod_scale,
    w_query,
    w_key,
    w_value,
    query_gain,
    key_gain,
    cache_keys,
    cache_values,
    owners,
    tile_mask,
):
    head_cols = w_query.shape[1]
    width = head_cols * lax.axis_size("tok")
    heads = tile_mask.shape[0]
    root = owners[owners.shape[0] - 1]
    joined = lax.all_gather(
        jnp.concatenate([w_key, w_value, w_query], axis=1), "group", axis=0, tiled=True
    )
    modulated = modulate(latents, timesteps[0], mod_shift, mod_scale)
    blocks = gather_tokens(modulated)
    cached_keys, cached_values = spread_cache(cache_keys, cache_values, root)
    order, count, slots = tile_lists(
        tile_mask, lax.axis_index("group") == 0, lax.axis_index("tok")
    )
    both = project(blocks, joined, 0, 2 * head_cols, 512)
    raw_key = both[:, :head_cols]
    value_rows = both[:, head_cols:].astype(jnp.bfloat16)
    earlier_values = from_behind(value_rows, "group", 1)
    key_squares = sum_over_tok(jnp.sum(raw_key * raw_key, axis=1))
    raw_query = project(blocks, joined, 2 * head_cols, head_cols, 512)
    key_rows = scaled_rows(raw_key, key_squares, width, key_gain)
    earlier_keys = from_behind(key_rows, "group", 1)
    query_squares = sum_over_tok(jnp.sum(raw_query * raw_query, axis=1))
    query_rows = scaled_rows(raw_query, query_squares, width, query_gain)
    parts = (cached_keys, cached_values, earlier_keys, earlier_values, key_rows, value_rows)
    return attend(query_rows, parts, order, count, slots, heads)


def solution(mesh):
    return jax.shard_map(
        local,
        mesh=mesh,
        in_specs=(
            P(("group", "tok"), None),
            P("group"),
            P(),
            P(),
            P("group", "tok"),
            P("group", "tok"),
            P("group", "tok"),
            P("tok"),
            P("tok"),
            P("group", "tok"),
            P("group", "tok"),
            P(),
            P("tok", None, None),
        ),
        out_specs=P("group", "tok"),
        check_vma=False,
    )
```

```python
import functools
import math

import jax
import jax.numpy as jnp
from jax import lax
from jax.experimental import pallas as pl
from jax.experimental.pallas import tpu as pltpu
from jax.sharding import PartitionSpec as P


EPSILON = 1e-06
TILE = 128
MOST = 8
FAR = -1e30
NY, NZ, NC, NX = 2, 8, 2, 4
SLOT_OF = (0, 1, 3, 5, 6, 7, 2, 4)
INTERPRET = False


def group_shift(value, dz=0, dc=0, dy=0):
    def at(y, z, c):
        return (y % NY) * NZ * NC + (z % NZ) * NC + c % NC

    route = [
        (at(y, z, c), at(y + dy, z + dz, c + dc))
        for y in range(NY)
        for z in range(NZ)
        for c in range(NC)
    ]
    return lax.ppermute(value, "group", route)


def tok_shift(value, dx=0, dy=0):
    route = [
        (x * 2 + y, ((x + dx) % NX) * 2 + (y + dy) % 2) for x in range(NX) for y in range(2)
    ]
    return lax.ppermute(value, "tok", route)


def from_behind(block, axis, distance):
    devices = range(lax.axis_size(axis))
    route = [(i - distance, i) for i in devices if i - distance in devices]
    return lax.ppermute(block, axis, route)


def modulate(rows_block, timestep, mod_shift, mod_scale):
    values = rows_block.astype(jnp.float32)
    width = values.shape[-1]
    centred = values - jnp.mean(values, axis=-1, keepdims=True)
    spread = jnp.mean(centred * centred, axis=-1, keepdims=True)
    normed = centred * lax.rsqrt(spread + EPSILON)
    freqs = jnp.exp(-math.log(10000.0) * jnp.arange(width, dtype=jnp.float32) / width)
    angles = timestep.astype(jnp.float32) * freqs
    return (
        normed * (1.0 + mod_scale + 0.5 * jnp.cos(angles)) + mod_shift + 0.5 * jnp.sin(angles)
    ).astype(jnp.bfloat16)


def scaled_rows(raw, squares, width, gain):
    return (raw * lax.rsqrt(squares / width + EPSILON)[:, None] * gain).astype(jnp.bfloat16)


def gather_tokens(own):
    half = own.shape[0] // 2

    def move(value, dx, dy=0):
        return tok_shift(value, dx, dy)

    beside = move(own, 0, 1)
    own_lo = move(own, 1)
    own_hi = move(own, -1)
    far_a = move(own_lo[:half], 1)
    far_b = move(own_hi[half:], -1)
    side_lo = move(beside, 1)
    side_hi = move(beside, -1)
    far_c = move(side_lo[:half], 1)
    far_d = move(side_hi[half:], -1)
    return (own, beside, own_lo, own_hi, side_lo, side_hi, far_a, far_b, far_c, far_d)


def fold_kernel(orders, held, *refs):
    came, out = refs[:-1], refs[-1]
    for slot in range(held.shape[0]):
        total = held[slot : slot + 1, :]
        for ref, order in zip(came, orders):
            total = total + ref[order[slot] : order[slot] + 1, :]
        out[slot : slot + 1, :] = total


def fold(value, shifts):
    orders = []
    for dx, dy in shifts:
        picks = [0] * (2 * NX)
        for n, slot in enumerate(SLOT_OF):
            picks[slot] = SLOT_OF[((n // 2 + dx) % NX) * 2 + (n % 2 + dy) % 2]
        orders.append(tuple(picks))
    came = [tok_shift(value, dx, dy) for dx, dy in shifts]
    return pl.pallas_call(
        functools.partial(fold_kernel, tuple(orders)),
        out_shape=jax.ShapeDtypeStruct(value.shape, value.dtype),
        interpret=INTERPRET,
        name="fold",
    )(value, *came)


def sum_over_tok(value):
    tiles = value.reshape(2 * NX, -1)
    pair = fold(tiles, ((0, 1),))
    return fold(pair, ((1, 0), (3, 0), (2, 0))).reshape(-1)


def swap_z(value, distance):
    def at(y, z, c):
        return y * NZ * NC + z * NC + c

    route = [
        (at(y, z, c), at(y, z ^ distance, c))
        for y in range(NY)
        for z in range(NZ)
        for c in range(NC)
    ]
    return lax.ppermute(value, "group", route)


def spread_cache(cache_keys, cache_values, root):
    me = lax.axis_index("group")
    moves = (
        (0, lambda v: group_shift(v, dc=1)),
        (4, lambda v: group_shift(v, dy=1)),
        (3, lambda v: swap_z(v, 4)),
        (2, lambda v: swap_z(v, 2)),
        (1, lambda v: swap_z(v, 1)),
    )
    low, high = cache_keys, cache_values
    for bit, move in moves:
        mine, theirs = (me >> bit) & 1, (root >> bit) & 1
        kept = jnp.where(mine == 1, high, low)
        sent = jnp.where(mine == 1, low, high)
        came = move(sent)
        held = jnp.where(mine == theirs, kept, came)
        half = held.shape[0] // 2
        low, high = held[:half], held[half:]
    for bit, move in moves[::-1]:
        mine = (me >> bit) & 1
        came = move(held)
        low, high = jnp.where(mine == 1, came, held), jnp.where(mine == 1, held, came)
        if bit:
            held = jnp.concatenate([low, high], axis=0)
    return low, high


def gather_weights(own):
    depth = own.shape[0]
    beside = group_shift(own, dy=1)
    pair = jnp.concatenate([own, beside], axis=0)
    low, high = [pair], [pair]
    for _ in range(1, NZ // 2):
        low.append(group_shift(low[-1], dz=1))
        high.append(group_shift(high[-1], dz=-1))
    own_half, beside_half = low[-1][:depth], high[-1][depth:]
    far_own = group_shift(own_half, dz=1)
    far_beside = group_shift(beside_half, dz=-1)
    me = lax.axis_index("group")
    y, z, c = me >> 4, (me >> 1) & (NZ - 1), me & 1

    def at(dy, dz, dc):
        return ((y ^ dy) << 4) | (((z + dz) & (NZ - 1)) << 1) | (c ^ dc)

    held = [(pair, ((0, 0), (1, 0)))]
    for k in range(1, NZ // 2):
        held.append((low[k], ((0, -k), (1, -k))))
        held.append((high[k], ((0, k), (1, k))))
    held.append((far_own, ((0, NZ // 2),)))
    held.append((far_beside, ((1, NZ // 2),)))
    pieces, places = [], []
    for dc in range(NC):
        for piece, where in held:
            pieces.append(piece if dc == 0 else group_shift(piece, dc=1))
            places += [at(dy, dz, dc) for dy, dz in where]
    return assemble(pieces, jnp.stack(places), depth)


def assemble_kernel(depth, places, *refs):
    pieces, out, sem = refs[:-2], refs[-2], refs[-1]
    copies = []
    for piece in pieces:
        for n in range(piece.shape[0] // depth):
            row = pl.multiple_of(places[len(copies)] * depth, depth)
            copies.append(
                pltpu.make_async_copy(
                    piece.at[pl.ds(n * depth, depth)],
                    out.at[pl.ds(row, depth)],
                    sem.at[len(copies)],
                )
            )
    for copy in copies:
        copy.start()
    for copy in copies:
        copy.wait()


def assemble(pieces, places, depth):
    columns = pieces[0].shape[1]
    rows = places.shape[0] * depth
    anywhere = pl.BlockSpec(memory_space=pl.ANY)
    return pl.pallas_call(
        functools.partial(assemble_kernel, depth),
        grid_spec=pltpu.PrefetchScalarGridSpec(
            num_scalar_prefetch=1,
            grid=(),
            in_specs=[anywhere] * len(pieces),
            out_specs=anywhere,
            scratch_shapes=[pltpu.SemaphoreType.DMA((places.shape[0],))],
        ),
        out_shape=jax.ShapeDtypeStruct((rows, columns), pieces[0].dtype),
        cost_estimate=pl.CostEstimate(
            flops=0, transcendentals=0, bytes_accessed=4 * rows * columns
        ),
        interpret=INTERPRET,
        name="assemble",
    )(places, *pieces)


def attend_kernel(
    heads, scale, order, count, slots, query, ck, cv, ek, ev, nk, nv, out, keys, values, sems
):
    span = ck.shape[0]
    parts = ((ck, cv), (ek, ev), (nk, nv))
    copies = []
    for n, (k_part, v_part) in enumerate(parts):
        rows = pl.ds(n * span, span)
        copies.append(pltpu.make_async_copy(k_part, keys.at[rows], sems.at[2 * n]))
        copies.append(pltpu.make_async_copy(v_part, values.at[rows], sems.at[2 * n + 1]))
    for copy in copies:
        copy.start()
    for copy in copies:
        copy.wait()
    tiles = span // TILE

    def few_tiles(first, pairs):
        low = lax.broadcasted_iota(jnp.int32, (1, 2 * TILE), 1) < TILE
        for h in range(heads):
            for i in (first, first + 1):
                one_tile(h, i, pairs, low)

    def one_tile(h, i, pairs, low):
        from_row = pl.multiple_of(slots[i] * TILE, TILE)
        to_row = pl.multiple_of(i * TILE, TILE)
        cols = pl.ds(h * TILE, TILE)
        at = h * tiles + i
        seen = count[at]
        q = query[pl.ds(from_row, TILE), cols]
        scores, vals = [], []
        for p in range(pairs):
            rows = [
                pl.ds(pl.multiple_of(order[at * MOST + 2 * p + s] * TILE, TILE), TILE)
                for s in range(2)
            ]
            k_pair = jnp.concatenate([keys[r, cols] for r in rows], axis=0)
            vals.append(jnp.concatenate([values[r, cols] for r in rows], axis=0))
            s = lax.dot_general(
                q, k_pair, (((1,), (1,)), ((), ())), preferred_element_type=jnp.float32
            )
            bias = jnp.where(
                low,
                jnp.where(2 * p < seen, 0.0, FAR),
                jnp.where(2 * p + 1 < seen, 0.0, FAR),
            )
            scores.append(s * scale + bias)
        top = scores[0]
        for s in scores[1:]:
            top = jnp.maximum(top, s)
        peak = jnp.max(top, axis=1, keepdims=True)
        total, summed = None, None
        for s, v in zip(scores, vals):
            probs = jnp.exp(s - peak)
            total = probs if total is None else total + probs
            added = jnp.dot(probs.astype(jnp.bfloat16), v, preferred_element_type=jnp.float32)
            summed = added if summed is None else summed + added
        denominator = jnp.sum(total, axis=1, keepdims=True)
        out[pl.ds(to_row, TILE), cols] = (summed / denominator).astype(jnp.bfloat16)

    @pl.loop(0, tiles // 2)
    def _(step):
        first = 2 * step
        most = count[first]
        for h in range(heads):
            for n in range(2):
                most = jnp.maximum(most, count[h * tiles + first + n])
        for pairs in range(2, MOST // 2 + 1):
            pl.when(jnp.maximum((most + 1) // 2, 2) == pairs)(functools.partial(few_tiles, first, pairs))


def attend(query, parts, order, count, slots, heads):
    rows, width = query.shape
    anywhere = pl.BlockSpec(memory_space=pl.ANY)
    whole = pl.BlockSpec(memory_space=pltpu.VMEM)
    return pl.pallas_call(
        functools.partial(attend_kernel, heads, 1.0 / math.sqrt(width // heads)),
        grid_spec=pltpu.PrefetchScalarGridSpec(
            num_scalar_prefetch=3,
            grid=(),
            in_specs=[whole] + [anywhere] * 6,
            out_specs=whole,
            scratch_shapes=[
                pltpu.VMEM((3 * rows, width), jnp.bfloat16),
                pltpu.VMEM((3 * rows, width), jnp.bfloat16),
                pltpu.SemaphoreType.DMA((6,)),
            ],
        ),
        out_shape=jax.ShapeDtypeStruct((rows, width), jnp.bfloat16),
        cost_estimate=pl.CostEstimate(
            flops=4 * rows * width * MOST * TILE,
            transcendentals=rows * heads * MOST * TILE,
            bytes_accessed=16 * rows * width,
        ),
        interpret=INTERPRET,
        name="attend",
    )(order, count, slots, query, *parts)


def tile_lists(tile_mask, is_first, tok):
    tiles, key_tiles = tile_mask.shape[1], tile_mask.shape[2]
    ids = jnp.arange(key_tiles, dtype=jnp.int32)
    earlier = (ids >= tiles) & (ids < 2 * tiles)
    allowed = jnp.where(earlier[None, None, :] & is_first, 0, tile_mask)
    count = jnp.sum(allowed, axis=-1)
    upto = (ids[None, :] <= ids[:, None]).astype(jnp.int32)
    rank = jnp.sum(allowed[:, :, None, :] * upto, axis=-1)
    places = jnp.arange(tiles, dtype=jnp.int32)
    step = (((places >> 1) - (tok >> 1)) & (NX - 1)) * 2 + ((places ^ tok) & 1)
    slots = sum(jnp.where(step == n, slot, 0) for n, slot in enumerate(SLOT_OF))
    physical = jnp.concatenate([places, tiles + slots, 2 * tiles + slots])
    turn = jnp.arange(1, MOST + 1, dtype=jnp.int32)
    picked = (rank[:, :, None, :] == turn[None, None, :, None]) & (allowed[:, :, None, :] > 0)
    order = jnp.sum(jnp.where(picked, physical, 0), axis=-1)
    return order.reshape(-1), count.reshape(-1), slots


def local(
    latents,
    timesteps,
    mod_shift,
    mod_scale,
    w_query,
    w_key,
    w_value,
    query_gain,
    key_gain,
    cache_keys,
    cache_values,
    owners,
    tile_mask,
):
    head_cols = w_query.shape[1]
    width = head_cols * lax.axis_size("tok")
    heads = tile_mask.shape[0]
    root = owners[owners.shape[0] - 1]
    modulated = modulate(latents, timesteps[0], mod_shift, mod_scale)
    joined = gather_weights(jnp.concatenate([w_key, w_value, w_query], axis=1))
    tokens = jnp.concatenate(gather_tokens(modulated), axis=0)
    cached_keys, cached_values = spread_cache(cache_keys, cache_values, root)
    order, count, slots = tile_lists(
        tile_mask, lax.axis_index("group") == 0, lax.axis_index("tok")
    )
    both = jnp.dot(tokens, joined[:, : 2 * head_cols], preferred_element_type=jnp.float32)
    raw_key = both[:, :head_cols]
    value_rows = both[:, head_cols:].astype(jnp.bfloat16)
    earlier_values = from_behind(value_rows, "group", 1)
    key_squares = sum_over_tok(jnp.sum(raw_key * raw_key, axis=1))
    raw_query = jnp.dot(tokens, joined[:, 2 * head_cols :], preferred_element_type=jnp.float32)
    key_rows = scaled_rows(raw_key, key_squares, width, key_gain)
    earlier_keys = from_behind(key_rows, "group", 1)
    query_squares = sum_over_tok(jnp.sum(raw_query * raw_query, axis=1))
    query_rows = scaled_rows(raw_query, query_squares, width, query_gain)
    parts = (cached_keys, cached_values, earlier_keys, earlier_values, key_rows, value_rows)
    return attend(query_rows, parts, order, count, slots, heads)


def solution(mesh):
    return jax.shard_map(
        local,
        mesh=mesh,
        in_specs=(
            P(("group", "tok"), None),
            P("group"),
            P(),
            P(),
            P("group", "tok"),
            P("group", "tok"),
            P("group", "tok"),
            P("tok"),
            P("tok"),
            P("group", "tok"),
            P("group", "tok"),
            P(),
            P("tok", None, None),
        ),
        out_specs=P("group", "tok"),
        check_vma=False,
    )
```

```python
import functools
import math

import jax
import jax.numpy as jnp
from jax import lax
from jax.experimental import pallas as pl
from jax.experimental.pallas import tpu as pltpu
from jax.sharding import PartitionSpec as P


EPSILON = 1e-06
TILE = 128
MOST = 8
FAR = -1e30
NY, NZ, NC, NX = 2, 8, 2, 4
SLOT_OF = (0, 1, 3, 5, 6, 7, 2, 4)
INTERPRET = False


def group_shift(value, dz=0, dc=0, dy=0):
    def at(y, z, c):
        return (y % NY) * NZ * NC + (z % NZ) * NC + c % NC

    route = [
        (at(y, z, c), at(y + dy, z + dz, c + dc))
        for y in range(NY)
        for z in range(NZ)
        for c in range(NC)
    ]
    return lax.ppermute(value, "group", route)


def tok_shift(value, dx=0, dy=0):
    route = [
        (x * 2 + y, ((x + dx) % NX) * 2 + (y + dy) % 2) for x in range(NX) for y in range(2)
    ]
    return lax.ppermute(value, "tok", route)


def from_behind(block, axis, distance):
    devices = range(lax.axis_size(axis))
    route = [(i - distance, i) for i in devices if i - distance in devices]
    return lax.ppermute(block, axis, route)


def modulate(rows_block, timestep, mod_shift, mod_scale):
    values = rows_block.astype(jnp.float32)
    width = values.shape[-1]
    centred = values - jnp.mean(values, axis=-1, keepdims=True)
    spread = jnp.mean(centred * centred, axis=-1, keepdims=True)
    normed = centred * lax.rsqrt(spread + EPSILON)
    freqs = jnp.exp(-math.log(10000.0) * jnp.arange(width, dtype=jnp.float32) / width)
    angles = timestep.astype(jnp.float32) * freqs
    return (
        normed * (1.0 + mod_scale + 0.5 * jnp.cos(angles)) + mod_shift + 0.5 * jnp.sin(angles)
    ).astype(jnp.bfloat16)


def scaled_rows(raw, squares, width, gain):
    return (raw * lax.rsqrt(squares / width + EPSILON)[:, None] * gain).astype(jnp.bfloat16)


def gather_tokens(own):
    half = own.shape[0] // 2

    def move(value, dx, dy=0):
        return tok_shift(value, dx, dy)

    beside = move(own, 0, 1)
    own_lo = move(own, 1)
    own_hi = move(own, -1)
    far_a = move(own_lo[:half], 1)
    far_b = move(own_hi[half:], -1)
    side_lo = move(beside, 1)
    side_hi = move(beside, -1)
    far_c = move(side_lo[:half], 1)
    far_d = move(side_hi[half:], -1)
    return (own, beside, own_lo, own_hi, side_lo, side_hi, far_a, far_b, far_c, far_d)


def fold_kernel(orders, held, *refs):
    came, out = refs[:-1], refs[-1]
    for slot in range(held.shape[0]):
        total = held[slot : slot + 1, :]
        for ref, order in zip(came, orders):
            total = total + ref[order[slot] : order[slot] + 1, :]
        out[slot : slot + 1, :] = total


def fold(value, shifts):
    tiles = 2 * NX
    orders, came = [], []
    for dx, dy in shifts:
        picks = [0] * tiles
        for n, slot in enumerate(SLOT_OF):
            picks[slot] = SLOT_OF[((n // 2 + dx) % NX) * 2 + (n % 2 + dy) % 2]
        orders.append(
            tuple(at * tiles + p for at in range(value.shape[0] // tiles) for p in picks)
        )
        came.append(tok_shift(value, dx, dy))
    return pl.pallas_call(
        functools.partial(fold_kernel, tuple(orders)),
        out_shape=jax.ShapeDtypeStruct(value.shape, value.dtype),
        interpret=INTERPRET,
        name="fold",
    )(value, *came)


def sum_over_tok(values):
    rows = values[0].shape[0]
    stacked = jnp.concatenate([v.reshape(2 * NX, -1) for v in values], axis=0)
    pair = fold(stacked, ((0, 1),))
    whole = fold(pair, ((1, 0), (3, 0), (2, 0)))
    return [whole[n * 2 * NX : (n + 1) * 2 * NX].reshape(rows) for n in range(len(values))]


def swap_z(value, distance):
    def at(y, z, c):
        return y * NZ * NC + z * NC + c

    route = [
        (at(y, z, c), at(y, z ^ distance, c))
        for y in range(NY)
        for z in range(NZ)
        for c in range(NC)
    ]
    return lax.ppermute(value, "group", route)


def spread_cache(cache_keys, cache_values, root):
    me = lax.axis_index("group")
    moves = (
        (0, lambda v: group_shift(v, dc=1)),
        (4, lambda v: group_shift(v, dy=1)),
        (3, lambda v: swap_z(v, 4)),
        (2, lambda v: swap_z(v, 2)),
        (1, lambda v: swap_z(v, 1)),
    )
    low, high = cache_keys, cache_values
    for bit, move in moves:
        mine, theirs = (me >> bit) & 1, (root >> bit) & 1
        kept = jnp.where(mine == 1, high, low)
        sent = jnp.where(mine == 1, low, high)
        came = move(sent)
        held = jnp.where(mine == theirs, kept, came)
        half = held.shape[0] // 2
        low, high = held[:half], held[half:]
    for bit, move in moves[::-1]:
        mine = (me >> bit) & 1
        came = move(held)
        if bit:
            low, high = jnp.where(mine == 1, came, held), jnp.where(mine == 1, held, came)
            held = jnp.concatenate([low, high], axis=0)
    return held, came


def attend_kernel(
    heads, scale, order, count, slots, query, ck, cv, ek, ev, nk, nv, out, keys, values, sems
):
    span = ck.shape[0]
    tiles = span // TILE

    def copies(parts):
        made = []
        for n, (part, target) in enumerate(parts):
            rows = pl.ds((n // 2) * span, span)
            made.append(pltpu.make_async_copy(part, target.at[rows], sems.at[n]))
        return made

    fresh = [(ek, keys), (ev, values), (nk, keys), (nv, values)]
    straight = copies([(ck, keys), (cv, values)] + fresh)
    crossed = copies([(cv, keys), (ck, values)] + fresh)

    @pl.when(slots[tiles] == 0)
    def _():
        for copy in straight[:2]:
            copy.start()

    @pl.when(slots[tiles] != 0)
    def _():
        for copy in crossed[:2]:
            copy.start()

    for copy in straight[2:]:
        copy.start()
    for copy in straight:
        copy.wait()

    def few_tiles(first, pairs):
        low = lax.broadcasted_iota(jnp.int32, (1, 2 * TILE), 1) < TILE
        for h in range(heads):
            for i in (first, first + 1):
                one_tile(h, i, pairs, low)

    def one_tile(h, i, pairs, low):
        from_row = pl.multiple_of(slots[i] * TILE, TILE)
        to_row = pl.multiple_of(i * TILE, TILE)
        cols = pl.ds(h * TILE, TILE)
        at = h * tiles + i
        seen = count[at]
        q = query[pl.ds(from_row, TILE), cols]
        scores, vals = [], []
        for p in range(pairs):
            rows = [
                pl.ds(pl.multiple_of(order[at * MOST + 2 * p + s] * TILE, TILE), TILE)
                for s in range(2)
            ]
            k_pair = jnp.concatenate([keys[r, cols] for r in rows], axis=0)
            vals.append(jnp.concatenate([values[r, cols] for r in rows], axis=0))
            s = lax.dot_general(
                q, k_pair, (((1,), (1,)), ((), ())), preferred_element_type=jnp.float32
            )
            bias = jnp.where(
                low,
                jnp.where(2 * p < seen, 0.0, FAR),
                jnp.where(2 * p + 1 < seen, 0.0, FAR),
            )
            scores.append(s * scale + bias)
        top = scores[0]
        for s in scores[1:]:
            top = jnp.maximum(top, s)
        peak = jnp.max(top, axis=1, keepdims=True)
        total, summed = None, None
        for s, v in zip(scores, vals):
            probs = jnp.exp(s - peak)
            total = probs if total is None else total + probs
            added = jnp.dot(probs.astype(jnp.bfloat16), v, preferred_element_type=jnp.float32)
            summed = added if summed is None else summed + added
        denominator = jnp.sum(total, axis=1, keepdims=True)
        out[pl.ds(to_row, TILE), cols] = (summed / denominator).astype(jnp.bfloat16)

    @pl.loop(0, tiles // 2)
    def _(step):
        first = 2 * step
        most = count[first]
        for h in range(heads):
            for n in range(2):
                most = jnp.maximum(most, count[h * tiles + first + n])
        few = MOST // 4
        pl.when(most <= 2 * few)(functools.partial(few_tiles, first, few))
        pl.when(most > 2 * few)(functools.partial(few_tiles, first, MOST // 2))


def attend(query, parts, order, count, slots, heads):
    rows, width = query.shape
    anywhere = pl.BlockSpec(memory_space=pl.ANY)
    whole = pl.BlockSpec(memory_space=pltpu.VMEM)
    return pl.pallas_call(
        functools.partial(attend_kernel, heads, 1.0 / math.sqrt(width // heads)),
        grid_spec=pltpu.PrefetchScalarGridSpec(
            num_scalar_prefetch=3,
            grid=(),
            in_specs=[whole] + [anywhere] * 6,
            out_specs=whole,
            scratch_shapes=[
                pltpu.VMEM((3 * rows, width), jnp.bfloat16),
                pltpu.VMEM((3 * rows, width), jnp.bfloat16),
                pltpu.SemaphoreType.DMA((6,)),
            ],
        ),
        out_shape=jax.ShapeDtypeStruct((rows, width), jnp.bfloat16),
        cost_estimate=pl.CostEstimate(
            flops=4 * rows * width * MOST * TILE,
            transcendentals=rows * heads * MOST * TILE,
            bytes_accessed=16 * rows * width,
        ),
        interpret=INTERPRET,
        name="attend",
    )(order, count, slots, query, *parts)


def tile_lists(tile_mask, is_first, tok):
    tiles, key_tiles = tile_mask.shape[1], tile_mask.shape[2]
    ids = jnp.arange(key_tiles, dtype=jnp.int32)
    earlier = (ids >= tiles) & (ids < 2 * tiles)
    allowed = jnp.where(earlier[None, None, :] & is_first, 0, tile_mask)
    count = jnp.sum(allowed, axis=-1)
    upto = (ids[None, :] <= ids[:, None]).astype(jnp.int32)
    rank = jnp.sum(allowed[:, :, None, :] * upto, axis=-1)
    places = jnp.arange(tiles, dtype=jnp.int32)
    step = (((places >> 1) - (tok >> 1)) & (NX - 1)) * 2 + ((places ^ tok) & 1)
    slots = sum(jnp.where(step == n, slot, 0) for n, slot in enumerate(SLOT_OF))
    physical = jnp.concatenate([places, tiles + slots, 2 * tiles + slots])
    turn = jnp.arange(1, MOST + 1, dtype=jnp.int32)
    picked = (rank[:, :, None, :] == turn[None, None, :, None]) & (allowed[:, :, None, :] > 0)
    order = jnp.sum(jnp.where(picked, physical, 0), axis=-1)
    core = jnp.reshape(lax.axis_index("group") & 1, (1,))
    return order.reshape(-1), count.reshape(-1), jnp.concatenate([slots, core])


def local(
    latents,
    timesteps,
    mod_shift,
    mod_scale,
    w_query,
    w_key,
    w_value,
    query_gain,
    key_gain,
    cache_keys,
    cache_values,
    owners,
    tile_mask,
):
    head_cols = w_query.shape[1]
    width = head_cols * lax.axis_size("tok")
    heads = tile_mask.shape[0]
    root = owners[owners.shape[0] - 1]
    modulated = modulate(latents, timesteps[0], mod_shift, mod_scale)
    joined = lax.all_gather(
        jnp.concatenate([w_query, w_key, w_value], axis=1), "group", axis=0, tiled=True
    )
    tokens = jnp.concatenate(gather_tokens(modulated), axis=0)
    held, crossed = spread_cache(cache_keys, cache_values, root)
    order, count, slots = tile_lists(
        tile_mask, lax.axis_index("group") == 0, lax.axis_index("tok")
    )
    both = lax.optimization_barrier(
        jnp.dot(tokens, joined[:, : 2 * head_cols], preferred_element_type=jnp.float32)
    )
    raw_query, raw_key = both[:, :head_cols], both[:, head_cols:]
    query_squares, key_squares = sum_over_tok(
        [jnp.sum(raw_query * raw_query, axis=1), jnp.sum(raw_key * raw_key, axis=1)]
    )
    value_rows = jnp.dot(
        tokens, joined[:, 2 * head_cols :], preferred_element_type=jnp.float32
    ).astype(jnp.bfloat16)
    earlier_values = from_behind(value_rows, "group", 1)
    key_rows = scaled_rows(raw_key, key_squares, width, key_gain)
    earlier_keys = from_behind(key_rows, "group", 1)
    query_rows = scaled_rows(raw_query, query_squares, width, query_gain)
    parts = (held, crossed, earlier_keys, earlier_values, key_rows, value_rows)
    return attend(query_rows, parts, order, count, slots, heads)


def solution(mesh):
    return jax.shard_map(
        local,
        mesh=mesh,
        in_specs=(
            P(("group", "tok"), None),
            P("group"),
            P(),
            P(),
            P("group", "tok"),
            P("group", "tok"),
            P("group", "tok"),
            P("tok"),
            P("tok"),
            P("group", "tok"),
            P("group", "tok"),
            P(),
            P("tok", None, None),
        ),
        out_specs=P("group", "tok"),
        check_vma=False,
    )
```

```python
import functools
import math

import jax
import jax.numpy as jnp
from jax import lax
from jax.experimental import pallas as pl
from jax.experimental.pallas import tpu as pltpu
from jax.sharding import PartitionSpec as P


EPSILON = 1e-06
TILE = 128
MOST = 8
FAR = -1e30
NY, NZ, NC, NX = 2, 8, 2, 4
SLOT_OF = (0, 1, 3, 5, 6, 7, 2, 4)
INTERPRET = False


def group_shift(value, dz=0, dc=0, dy=0):
    def at(y, z, c):
        return (y % NY) * NZ * NC + (z % NZ) * NC + c % NC

    route = [
        (at(y, z, c), at(y + dy, z + dz, c + dc))
        for y in range(NY)
        for z in range(NZ)
        for c in range(NC)
    ]
    return lax.ppermute(value, "group", route)


def tok_shift(value, dx=0, dy=0):
    route = [
        (x * 2 + y, ((x + dx) % NX) * 2 + (y + dy) % 2) for x in range(NX) for y in range(2)
    ]
    return lax.ppermute(value, "tok", route)


def from_behind(block, axis, distance):
    devices = range(lax.axis_size(axis))
    route = [(i - distance, i) for i in devices if i - distance in devices]
    return lax.ppermute(block, axis, route)


def modulate(rows_block, timestep, mod_shift, mod_scale):
    values = rows_block.astype(jnp.float32)
    width = values.shape[-1]
    centred = values - jnp.mean(values, axis=-1, keepdims=True)
    spread = jnp.mean(centred * centred, axis=-1, keepdims=True)
    normed = centred * lax.rsqrt(spread + EPSILON)
    freqs = jnp.exp(-math.log(10000.0) * jnp.arange(width, dtype=jnp.float32) / width)
    angles = timestep.astype(jnp.float32) * freqs
    return (
        normed * (1.0 + mod_scale + 0.5 * jnp.cos(angles)) + mod_shift + 0.5 * jnp.sin(angles)
    ).astype(jnp.bfloat16)


def scaled_rows(raw, squares, width, gain):
    return (raw * lax.rsqrt(squares / width + EPSILON)[:, None] * gain).astype(jnp.bfloat16)


def gather_tokens(own):
    half = own.shape[0] // 2

    def move(value, dx, dy=0):
        return tok_shift(value, dx, dy)

    beside = move(own, 0, 1)
    own_lo = move(own, 1)
    own_hi = move(own, -1)
    far_a = move(own_lo[:half], 1)
    far_b = move(own_hi[half:], -1)
    side_lo = move(beside, 1)
    side_hi = move(beside, -1)
    far_c = move(side_lo[:half], 1)
    far_d = move(side_hi[half:], -1)
    return (own, beside, own_lo, own_hi, side_lo, side_hi, far_a, far_b, far_c, far_d)


def fold_kernel(orders, held, *refs):
    came, out = refs[:-1], refs[-1]
    for slot in range(held.shape[0]):
        total = held[slot : slot + 1, :]
        for ref, order in zip(came, orders):
            total = total + ref[order[slot] : order[slot] + 1, :]
        out[slot : slot + 1, :] = total


def fold(value, shifts):
    tiles = 2 * NX
    orders, came = [], []
    for dx, dy in shifts:
        picks = [0] * tiles
        for n, slot in enumerate(SLOT_OF):
            picks[slot] = SLOT_OF[((n // 2 + dx) % NX) * 2 + (n % 2 + dy) % 2]
        orders.append(
            tuple(at * tiles + p for at in range(value.shape[0] // tiles) for p in picks)
        )
        came.append(tok_shift(value, dx, dy))
    return pl.pallas_call(
        functools.partial(fold_kernel, tuple(orders)),
        out_shape=jax.ShapeDtypeStruct(value.shape, value.dtype),
        interpret=INTERPRET,
        name="fold",
    )(value, *came)


def sum_over_tok(values):
    rows = values[0].shape[0]
    stacked = jnp.concatenate([v.reshape(2 * NX, -1) for v in values], axis=0)
    pair = fold(stacked, ((0, 1),))
    whole = fold(pair, ((1, 0), (3, 0), (2, 0)))
    return [whole[n * 2 * NX : (n + 1) * 2 * NX].reshape(rows) for n in range(len(values))]


def swap_z(value, distance):
    def at(y, z, c):
        return y * NZ * NC + z * NC + c

    route = [
        (at(y, z, c), at(y, z ^ distance, c))
        for y in range(NY)
        for z in range(NZ)
        for c in range(NC)
    ]
    return lax.ppermute(value, "group", route)


def spread_cache(cache_keys, cache_values, root):
    me = lax.axis_index("group")
    moves = (
        (0, lambda v: group_shift(v, dc=1)),
        (4, lambda v: group_shift(v, dy=1)),
        (1, lambda v: swap_z(v, 1)),
        (2, lambda v: swap_z(v, 2)),
        (3, lambda v: swap_z(v, 4)),
    )
    low, high = cache_keys, cache_values
    for bit, move in moves:
        mine, theirs = (me >> bit) & 1, (root >> bit) & 1
        kept = jnp.where(mine == 1, high, low)
        sent = jnp.where(mine == 1, low, high)
        came = move(sent)
        held = jnp.where(mine == theirs, kept, came)
        half = held.shape[0] // 2
        low, high = held[:half], held[half:]
    for bit, move in moves[::-1]:
        mine = (me >> bit) & 1
        came = move(held)
        if bit:
            low, high = jnp.where(mine == 1, came, held), jnp.where(mine == 1, held, came)
            held = jnp.concatenate([low, high], axis=0)
    return held, came


def attend_kernel(
    heads, scale, order, count, slots, query, ck, cv, ek, ev, nk, nv, out, keys, values, sems
):
    span = ck.shape[0]
    tiles = span // TILE

    def copies(parts):
        made = []
        for n, (part, target) in enumerate(parts):
            rows = pl.ds((n // 2) * span, span)
            made.append(pltpu.make_async_copy(part, target.at[rows], sems.at[n]))
        return made

    fresh = [(ek, keys), (ev, values), (nk, keys), (nv, values)]
    straight = copies([(ck, keys), (cv, values)] + fresh)
    crossed = copies([(cv, keys), (ck, values)] + fresh)

    @pl.when(slots[tiles] == 0)
    def _():
        for copy in straight[:2]:
            copy.start()

    @pl.when(slots[tiles] != 0)
    def _():
        for copy in crossed[:2]:
            copy.start()

    for copy in straight[2:]:
        copy.start()
    for copy in straight:
        copy.wait()

    def few_tiles(first, pairs):
        low = lax.broadcasted_iota(jnp.int32, (1, 2 * TILE), 1) < TILE
        for h in range(heads):
            for i in (first, first + 1):
                one_tile(h, i, pairs, low)

    def one_tile(h, i, pairs, low):
        from_row = pl.multiple_of(slots[i] * TILE, TILE)
        to_row = pl.multiple_of(i * TILE, TILE)
        cols = pl.ds(h * TILE, TILE)
        at = h * tiles + i
        seen = count[at]
        q = query[pl.ds(from_row, TILE), cols]
        scores, vals = [], []
        for p in range(pairs):
            rows = [
                pl.ds(pl.multiple_of(order[at * MOST + 2 * p + s] * TILE, TILE), TILE)
                for s in range(2)
            ]
            k_pair = jnp.concatenate([keys[r, cols] for r in rows], axis=0)
            vals.append(jnp.concatenate([values[r, cols] for r in rows], axis=0))
            s = lax.dot_general(
                q, k_pair, (((1,), (1,)), ((), ())), preferred_element_type=jnp.float32
            )
            bias = jnp.where(
                low,
                jnp.where(2 * p < seen, 0.0, FAR),
                jnp.where(2 * p + 1 < seen, 0.0, FAR),
            )
            scores.append(s * scale + bias)
        top = scores[0]
        for s in scores[1:]:
            top = jnp.maximum(top, s)
        peak = jnp.max(top, axis=1, keepdims=True)
        total, summed = None, None
        for s, v in zip(scores, vals):
            probs = jnp.exp(s - peak)
            total = probs if total is None else total + probs
            added = jnp.dot(probs.astype(jnp.bfloat16), v, preferred_element_type=jnp.float32)
            summed = added if summed is None else summed + added
        denominator = jnp.sum(total, axis=1, keepdims=True)
        out[pl.ds(to_row, TILE), cols] = (summed / denominator).astype(jnp.bfloat16)

    @pl.loop(0, tiles // 2)
    def _(step):
        first = 2 * step
        few_tiles(first, MOST // 2)


def attend(query, parts, order, count, slots, heads):
    rows, width = query.shape
    anywhere = pl.BlockSpec(memory_space=pl.ANY)
    whole = pl.BlockSpec(memory_space=pltpu.VMEM)
    return pl.pallas_call(
        functools.partial(attend_kernel, heads, 1.0 / math.sqrt(width // heads)),
        grid_spec=pltpu.PrefetchScalarGridSpec(
            num_scalar_prefetch=3,
            grid=(),
            in_specs=[whole] + [anywhere] * 6,
            out_specs=whole,
            scratch_shapes=[
                pltpu.VMEM((3 * rows, width), jnp.bfloat16),
                pltpu.VMEM((3 * rows, width), jnp.bfloat16),
                pltpu.SemaphoreType.DMA((6,)),
            ],
        ),
        out_shape=jax.ShapeDtypeStruct((rows, width), jnp.bfloat16),
        cost_estimate=pl.CostEstimate(
            flops=4 * rows * width * MOST * TILE,
            transcendentals=rows * heads * MOST * TILE,
            bytes_accessed=16 * rows * width,
        ),
        interpret=INTERPRET,
        name="attend",
    )(order, count, slots, query, *parts)


def tile_lists(tile_mask, is_first, tok):
    tiles, key_tiles = tile_mask.shape[1], tile_mask.shape[2]
    ids = jnp.arange(key_tiles, dtype=jnp.int32)
    earlier = (ids >= tiles) & (ids < 2 * tiles)
    allowed = jnp.where(earlier[None, None, :] & is_first, 0, tile_mask)
    count = jnp.sum(allowed, axis=-1)
    upto = (ids[None, :] <= ids[:, None]).astype(jnp.int32)
    rank = jnp.sum(allowed[:, :, None, :] * upto, axis=-1)
    places = jnp.arange(tiles, dtype=jnp.int32)
    step = (((places >> 1) - (tok >> 1)) & (NX - 1)) * 2 + ((places ^ tok) & 1)
    slots = sum(jnp.where(step == n, slot, 0) for n, slot in enumerate(SLOT_OF))
    physical = jnp.concatenate([places, tiles + slots, 2 * tiles + slots])
    turn = jnp.arange(1, MOST + 1, dtype=jnp.int32)
    picked = (rank[:, :, None, :] == turn[None, None, :, None]) & (allowed[:, :, None, :] > 0)
    order = jnp.sum(jnp.where(picked, physical, 0), axis=-1)
    core = jnp.reshape(lax.axis_index("group") & 1, (1,))
    return order.reshape(-1), count.reshape(-1), jnp.concatenate([slots, core])


def local(
    latents,
    timesteps,
    mod_shift,
    mod_scale,
    w_query,
    w_key,
    w_value,
    query_gain,
    key_gain,
    cache_keys,
    cache_values,
    owners,
    tile_mask,
):
    head_cols = w_query.shape[1]
    width = head_cols * lax.axis_size("tok")
    heads = tile_mask.shape[0]
    root = owners[owners.shape[0] - 1]
    modulated = modulate(latents, timesteps[0], mod_shift, mod_scale)
    own_w = jnp.concatenate([w_query, w_key, w_value], axis=1)
    beside_w = group_shift(own_w, dy=1)
    planes = [[y * NZ * NC + n for n in range(NZ * NC)] for y in range(NY)]
    weights = []
    for w in (own_w, beside_w):
        weights.append(
            lax.all_gather(w, "group", axis_index_groups=planes, axis=0, tiled=True)
        )
    depth = weights[0].shape[0]
    modulated = modulate(latents, timesteps[0], mod_shift, mod_scale)
    swapped = jnp.concatenate([modulated[:, depth:], modulated[:, :depth]], axis=1)
    modulated = jnp.where(lax.axis_index("group") < NZ * NC, modulated, swapped)
    tokens = jnp.concatenate(gather_tokens(modulated), axis=0)

    def projected(first, last):
        parts = [
            jnp.dot(
                tokens[:, n * depth : (n + 1) * depth],
                w[:, first:last],
                preferred_element_type=jnp.float32,
            )
            for n, w in enumerate(weights)
        ]
        return parts[0] + parts[1]

    held, crossed = spread_cache(cache_keys, cache_values, root)
    order, count, slots = tile_lists(
        tile_mask, lax.axis_index("group") == 0, lax.axis_index("tok")
    )
    both = lax.optimization_barrier(projected(0, 2 * head_cols))
    raw_query, raw_key = both[:, :head_cols], both[:, head_cols:]
    query_squares, key_squares = sum_over_tok(
        [jnp.sum(raw_query * raw_query, axis=1), jnp.sum(raw_key * raw_key, axis=1)]
    )
    value_rows = projected(2 * head_cols, 3 * head_cols).astype(jnp.bfloat16)
    earlier_values = from_behind(value_rows, "group", 1)
    key_rows = scaled_rows(raw_key, key_squares, width, key_gain)
    earlier_keys = from_behind(key_rows, "group", 1)
    query_rows = scaled_rows(raw_query, query_squares, width, query_gain)
    parts = (held, crossed, earlier_keys, earlier_values, key_rows, value_rows)
    return attend(query_rows, parts, order, count, slots, heads)


def solution(mesh):
    return jax.shard_map(
        local,
        mesh=mesh,
        in_specs=(
            P(("group", "tok"), None),
            P("group"),
            P(),
            P(),
            P("group", "tok"),
            P("group", "tok"),
            P("group", "tok"),
            P("tok"),
            P("tok"),
            P("group", "tok"),
            P("group", "tok"),
            P(),
            P("tok", None, None),
        ),
        out_specs=P("group", "tok"),
        check_vma=False,
    )
```

```python
import functools
import math

import jax
import jax.numpy as jnp
from jax import lax
from jax.experimental import pallas as pl
from jax.experimental.pallas import tpu as pltpu
from jax.sharding import PartitionSpec as P


EPSILON = 1e-06
TILE = 128
MOST = 8
FAR = -1e30
NY, NZ, NC, NX = 2, 8, 2, 4
SLOT_OF = (0, 1, 3, 5, 6, 7, 2, 4)
INTERPRET = False


def group_shift(value, dz=0, dc=0, dy=0):
    def at(y, z, c):
        return (y % NY) * NZ * NC + (z % NZ) * NC + c % NC

    route = [
        (at(y, z, c), at(y + dy, z + dz, c + dc))
        for y in range(NY)
        for z in range(NZ)
        for c in range(NC)
    ]
    return lax.ppermute(value, "group", route)


def tok_shift(value, dx=0, dy=0):
    route = [
        (x * 2 + y, ((x + dx) % NX) * 2 + (y + dy) % 2) for x in range(NX) for y in range(2)
    ]
    return lax.ppermute(value, "tok", route)


def from_behind(block, axis, distance):
    devices = range(lax.axis_size(axis))
    route = [(i - distance, i) for i in devices if i - distance in devices]
    return lax.ppermute(block, axis, route)


def modulate(rows_block, timestep, mod_shift, mod_scale):
    values = rows_block.astype(jnp.float32)
    width = values.shape[-1]
    centred = values - jnp.mean(values, axis=-1, keepdims=True)
    spread = jnp.mean(centred * centred, axis=-1, keepdims=True)
    normed = centred * lax.rsqrt(spread + EPSILON)
    freqs = jnp.exp(-math.log(10000.0) * jnp.arange(width, dtype=jnp.float32) / width)
    angles = timestep.astype(jnp.float32) * freqs
    return (
        normed * (1.0 + mod_scale + 0.5 * jnp.cos(angles)) + mod_shift + 0.5 * jnp.sin(angles)
    ).astype(jnp.bfloat16)


def scaled_rows(raw, squares, width, gain):
    return (raw * lax.rsqrt(squares / width + EPSILON)[:, None] * gain).astype(jnp.bfloat16)


def gather_tokens(own):
    half = own.shape[0] // 2

    def move(value, dx, dy=0):
        return tok_shift(value, dx, dy)

    beside = move(own, 0, 1)
    own_lo = move(own, 1)
    own_hi = move(own, -1)
    far_a = move(own_lo[:half], 1)
    far_b = move(own_hi[half:], -1)
    side_lo = move(beside, 1)
    side_hi = move(beside, -1)
    far_c = move(side_lo[:half], 1)
    far_d = move(side_hi[half:], -1)
    return (own, beside, own_lo, own_hi, side_lo, side_hi, far_a, far_b, far_c, far_d)


def fold_kernel(orders, held, *refs):
    came, out = refs[:-1], refs[-1]
    for slot in range(held.shape[0]):
        total = held[slot : slot + 1, :]
        for ref, order in zip(came, orders):
            total = total + ref[order[slot] : order[slot] + 1, :]
        out[slot : slot + 1, :] = total


def fold(value, shifts):
    tiles = 2 * NX
    orders, came = [], []
    for dx, dy in shifts:
        picks = [0] * tiles
        for n, slot in enumerate(SLOT_OF):
            picks[slot] = SLOT_OF[((n // 2 + dx) % NX) * 2 + (n % 2 + dy) % 2]
        orders.append(
            tuple(at * tiles + p for at in range(value.shape[0] // tiles) for p in picks)
        )
        came.append(tok_shift(value, dx, dy))
    return pl.pallas_call(
        functools.partial(fold_kernel, tuple(orders)),
        out_shape=jax.ShapeDtypeStruct(value.shape, value.dtype),
        interpret=INTERPRET,
        name="fold",
    )(value, *came)


def sum_over_tok(values):
    rows = values[0].shape[0]
    stacked = jnp.concatenate([v.reshape(2 * NX, -1) for v in values], axis=0)
    pair = fold(stacked, ((0, 1),))
    whole = fold(pair, ((1, 0), (3, 0), (2, 0)))
    return [whole[n * 2 * NX : (n + 1) * 2 * NX].reshape(rows) for n in range(len(values))]


def swap_z(value, distance):
    def at(y, z, c):
        return y * NZ * NC + z * NC + c

    route = [
        (at(y, z, c), at(y, z ^ distance, c))
        for y in range(NY)
        for z in range(NZ)
        for c in range(NC)
    ]
    return lax.ppermute(value, "group", route)


def spread_cache(cache_keys, cache_values, root, after):
    me = lax.axis_index("group")
    moves = (
        (0, lambda v: group_shift(v, dc=1)),
        (4, lambda v: group_shift(v, dy=1)),
        (1, lambda v: swap_z(v, 1)),
        (2, lambda v: swap_z(v, 2)),
        (3, lambda v: swap_z(v, 4)),
    )
    low, high = cache_keys, cache_values
    for n, (bit, move) in enumerate(moves):
        mine, theirs = (me >> bit) & 1, (root >> bit) & 1
        kept = jnp.where(mine == 1, high, low)
        sent = jnp.where(mine == 1, low, high)
        came = move(sent)
        if n == 1:
            came, _ = lax.optimization_barrier((came, after))
        held = jnp.where(mine == theirs, kept, came)
        half = held.shape[0] // 2
        low, high = held[:half], held[half:]
    for bit, move in moves[::-1]:
        mine = (me >> bit) & 1
        came = move(held)
        if bit:
            low, high = jnp.where(mine == 1, came, held), jnp.where(mine == 1, held, came)
            held = jnp.concatenate([low, high], axis=0)
    return held, came


def attend_kernel(
    heads, scale, order, count, slots, query, ck, cv, ek0, ek1, ev0, ev1, nk, nv, *rest
):
    out, keys, values, sems = rest
    span = ck.shape[0]
    tiles, half = span // TILE, span // 2

    def copies(parts):
        made = []
        for n, (part, target, row) in enumerate(parts):
            rows = pl.ds(row, part.shape[0])
            made.append(pltpu.make_async_copy(part, target.at[rows], sems.at[n]))
        return made

    fresh = [
        (ek0, keys, span),
        (ek1, keys, span + half),
        (ev0, values, span),
        (ev1, values, span + half),
        (nk, keys, 2 * span),
        (nv, values, 2 * span),
    ]
    straight = copies([(ck, keys, 0), (cv, values, 0)] + fresh)
    crossed = copies([(cv, keys, 0), (ck, values, 0)] + fresh)

    @pl.when(slots[tiles] == 0)
    def _():
        for copy in straight[:2]:
            copy.start()

    @pl.when(slots[tiles] != 0)
    def _():
        for copy in crossed[:2]:
            copy.start()

    for copy in straight[2:]:
        copy.start()
    for copy in straight:
        copy.wait()

    def all_heads(i, pairs):
        low = lax.broadcasted_iota(jnp.int32, (1, 2 * TILE), 1) < TILE
        for h in range(heads):
            one_tile(h, i, pairs, low)

    def one_tile(h, i, pairs, low):
        from_row = pl.multiple_of(slots[i] * TILE, TILE)
        to_row = pl.multiple_of(i * TILE, TILE)
        cols = pl.ds(h * TILE, TILE)
        at = h * tiles + i
        seen = count[at]
        q = query[pl.ds(from_row, TILE), cols]
        scores, vals = [], []
        for p in range(pairs):
            rows = [
                pl.ds(pl.multiple_of(order[at * MOST + 2 * p + s] * TILE, TILE), TILE)
                for s in range(2)
            ]
            k_pair = jnp.concatenate([keys[r, cols] for r in rows], axis=0)
            vals.append(jnp.concatenate([values[r, cols] for r in rows], axis=0))
            s = lax.dot_general(
                q, k_pair, (((1,), (1,)), ((), ())), preferred_element_type=jnp.float32
            )
            bias = jnp.where(
                low,
                jnp.where(2 * p < seen, 0.0, FAR),
                jnp.where(2 * p + 1 < seen, 0.0, FAR),
            )
            scores.append(s * scale + bias)
        top = scores[0]
        for s in scores[1:]:
            top = jnp.maximum(top, s)
        peak = jnp.max(top, axis=1, keepdims=True)
        total, summed = None, None
        for s, v in zip(scores, vals):
            probs = jnp.exp(s - peak)
            total = probs if total is None else total + probs
            added = jnp.dot(probs.astype(jnp.bfloat16), v, preferred_element_type=jnp.float32)
            summed = added if summed is None else summed + added
        denominator = jnp.sum(total, axis=1, keepdims=True)
        out[pl.ds(to_row, TILE), cols] = (summed / denominator).astype(jnp.bfloat16)

    @pl.loop(0, tiles)
    def _(i):
        all_heads(i, MOST // 2)


def attend(query, parts, order, count, slots, heads):
    rows, width = query.shape
    anywhere = pl.BlockSpec(memory_space=pl.ANY)
    whole = pl.BlockSpec(memory_space=pltpu.VMEM)
    return pl.pallas_call(
        functools.partial(attend_kernel, heads, 1.0 / math.sqrt(width // heads)),
        grid_spec=pltpu.PrefetchScalarGridSpec(
            num_scalar_prefetch=3,
            grid=(),
            in_specs=[whole] + [anywhere] * len(parts),
            out_specs=whole,
            scratch_shapes=[
                pltpu.VMEM((3 * rows, width), jnp.bfloat16),
                pltpu.VMEM((3 * rows, width), jnp.bfloat16),
                pltpu.SemaphoreType.DMA((len(parts),)),
            ],
        ),
        out_shape=jax.ShapeDtypeStruct((rows, width), jnp.bfloat16),
        cost_estimate=pl.CostEstimate(
            flops=4 * rows * width * MOST * TILE,
            transcendentals=rows * heads * MOST * TILE,
            bytes_accessed=16 * rows * width,
        ),
        interpret=INTERPRET,
        name="attend",
    )(order, count, slots, query, *parts)


def tile_lists(tile_mask, is_first, tok):
    tiles, key_tiles = tile_mask.shape[1], tile_mask.shape[2]
    ids = jnp.arange(key_tiles, dtype=jnp.int32)
    earlier = (ids >= tiles) & (ids < 2 * tiles)
    allowed = jnp.where(earlier[None, None, :] & is_first, 0, tile_mask)
    count = jnp.sum(allowed, axis=-1)
    upto = (ids[None, :] <= ids[:, None]).astype(jnp.int32)
    rank = jnp.sum(allowed[:, :, None, :] * upto, axis=-1)
    places = jnp.arange(tiles, dtype=jnp.int32)
    step = (((places >> 1) - (tok >> 1)) & (NX - 1)) * 2 + ((places ^ tok) & 1)
    slots = sum(jnp.where(step == n, slot, 0) for n, slot in enumerate(SLOT_OF))
    physical = jnp.concatenate([places, tiles + slots, 2 * tiles + slots])
    turn = jnp.arange(1, MOST + 1, dtype=jnp.int32)
    picked = (rank[:, :, None, :] == turn[None, None, :, None]) & (allowed[:, :, None, :] > 0)
    order = jnp.sum(jnp.where(picked, physical, 0), axis=-1)
    core = jnp.reshape(lax.axis_index("group") & 1, (1,))
    return order.reshape(-1), count.reshape(-1), jnp.concatenate([slots, core])


def local(
    latents,
    timesteps,
    mod_shift,
    mod_scale,
    w_query,
    w_key,
    w_value,
    query_gain,
    key_gain,
    cache_keys,
    cache_values,
    owners,
    tile_mask,
):
    head_cols = w_query.shape[1]
    width = head_cols * lax.axis_size("tok")
    heads = tile_mask.shape[0]
    root = owners[owners.shape[0] - 1]
    modulated = modulate(latents, timesteps[0], mod_shift, mod_scale)
    own_w = jnp.concatenate([w_query, w_key, w_value], axis=1)
    beside_w = group_shift(own_w, dy=1)
    planes = [[y * NZ * NC + n for n in range(NZ * NC)] for y in range(NY)]
    weights = []
    for w in (own_w, beside_w):
        weights.append(
            lax.all_gather(w, "group", axis_index_groups=planes, axis=0, tiled=True)
        )
    depth = weights[0].shape[0]
    modulated = modulate(latents, timesteps[0], mod_shift, mod_scale)
    swapped = jnp.concatenate([modulated[:, depth:], modulated[:, :depth]], axis=1)
    modulated = jnp.where(lax.axis_index("group") < NZ * NC, modulated, swapped)
    blocks = gather_tokens(modulated)
    tokens = jnp.concatenate(blocks, axis=0)

    def projected(first, last):
        parts = []
        for n, w in enumerate(weights):
            parts.append(
                jnp.dot(
                    tokens[:, n * depth : (n + 1) * depth],
                    w[:, first:last],
                    preferred_element_type=jnp.float32,
                )
            )
        return parts[0] + parts[1]

    held, crossed = spread_cache(cache_keys, cache_values, root, blocks[1])
    order, count, slots = tile_lists(
        tile_mask, lax.axis_index("group") == 0, lax.axis_index("tok")
    )
    both = lax.optimization_barrier(projected(0, 2 * head_cols))
    raw_query, raw_key = both[:, :head_cols], both[:, head_cols:]
    query_squares, key_squares = sum_over_tok(
        [jnp.sum(raw_query * raw_query, axis=1), jnp.sum(raw_key * raw_key, axis=1)]
    )
    value_rows = projected(2 * head_cols, 3 * head_cols).astype(jnp.bfloat16)
    half = value_rows.shape[0] // 2
    earlier_values = []
    for n in range(2):
        earlier_values.append(from_behind(value_rows[n * half : (n + 1) * half], "group", 1))
    key_rows = scaled_rows(raw_key, key_squares, width, key_gain)
    earlier_keys = []
    for n in range(2):
        earlier_keys.append(from_behind(key_rows[n * half : (n + 1) * half], "group", 1))
    query_rows = scaled_rows(raw_query, query_squares, width, query_gain)
    parts = (held, crossed, *earlier_keys, *earlier_values, key_rows, value_rows)
    return attend(query_rows, parts, order, count, slots, heads)


def solution(mesh):
    return jax.shard_map(
        local,
        mesh=mesh,
        in_specs=(
            P(("group", "tok"), None),
            P("group"),
            P(),
            P(),
            P("group", "tok"),
            P("group", "tok"),
            P("group", "tok"),
            P("tok"),
            P("tok"),
            P("group", "tok"),
            P("group", "tok"),
            P(),
            P("tok", None, None),
        ),
        out_specs=P("group", "tok"),
        check_vma=False,
    )
```

```python
import functools
import math

import jax
import jax.numpy as jnp
from jax import lax
from jax.experimental import pallas as pl
from jax.experimental.pallas import tpu as pltpu
from jax.sharding import PartitionSpec as P


EPSILON = 1e-06
TILE = 128
MOST = 8
FAR = -1e30
NY, NZ, NC, NX = 2, 8, 2, 4
SLOT_OF = (0, 1, 3, 5, 6, 7, 2, 4)
INTERPRET = False


def group_shift(value, dz=0, dc=0, dy=0):
    def at(y, z, c):
        return (y % NY) * NZ * NC + (z % NZ) * NC + c % NC

    route = [
        (at(y, z, c), at(y + dy, z + dz, c + dc))
        for y in range(NY)
        for z in range(NZ)
        for c in range(NC)
    ]
    return lax.ppermute(value, "group", route)


def tok_shift(value, dx=0, dy=0):
    route = [
        (x * 2 + y, ((x + dx) % NX) * 2 + (y + dy) % 2) for x in range(NX) for y in range(2)
    ]
    return lax.ppermute(value, "tok", route)


def from_behind(block, axis, distance):
    devices = range(lax.axis_size(axis))
    route = [(i - distance, i) for i in devices if i - distance in devices]
    return lax.ppermute(block, axis, route)


def modulate(rows_block, timestep, mod_shift, mod_scale):
    values = rows_block.astype(jnp.float32)
    width = values.shape[-1]
    centred = values - jnp.mean(values, axis=-1, keepdims=True)
    spread = jnp.mean(centred * centred, axis=-1, keepdims=True)
    normed = centred * lax.rsqrt(spread + EPSILON)
    freqs = jnp.exp(-math.log(10000.0) * jnp.arange(width, dtype=jnp.float32) / width)
    angles = timestep.astype(jnp.float32) * freqs
    return (
        normed * (1.0 + mod_scale + 0.5 * jnp.cos(angles)) + mod_shift + 0.5 * jnp.sin(angles)
    ).astype(jnp.bfloat16)


def scaled_rows(raw, squares, width, gain):
    return (raw * lax.rsqrt(squares / width + EPSILON)[:, None] * gain).astype(jnp.bfloat16)


def gather_tokens(own):
    half = own.shape[0] // 2

    def move(value, dx, dy=0):
        return tok_shift(value, dx, dy)

    beside = move(own, 0, 1)
    own_lo = move(own, 1)
    own_hi = move(own, -1)
    far_a = move(own_lo[:half], 1)
    far_b = move(own_hi[half:], -1)
    side_lo = move(beside, 1)
    side_hi = move(beside, -1)
    far_c = move(side_lo[:half], 1)
    far_d = move(side_hi[half:], -1)
    return (own, beside, own_lo, own_hi, side_lo, side_hi, far_a, far_b, far_c, far_d)


def fold_kernel(orders, held, *refs):
    came, out = refs[:-1], refs[-1]
    for slot in range(held.shape[0]):
        total = held[slot : slot + 1, :]
        for ref, order in zip(came, orders):
            total = total + ref[order[slot] : order[slot] + 1, :]
        out[slot : slot + 1, :] = total


def fold(value, shifts):
    tiles = 2 * NX
    orders, came = [], []
    for dx, dy in shifts:
        picks = [0] * tiles
        for n, slot in enumerate(SLOT_OF):
            picks[slot] = SLOT_OF[((n // 2 + dx) % NX) * 2 + (n % 2 + dy) % 2]
        orders.append(
            tuple(at * tiles + p for at in range(value.shape[0] // tiles) for p in picks)
        )
        came.append(tok_shift(value, dx, dy))
    return pl.pallas_call(
        functools.partial(fold_kernel, tuple(orders)),
        out_shape=jax.ShapeDtypeStruct(value.shape, value.dtype),
        interpret=INTERPRET,
        name="fold",
    )(value, *came)


def sum_over_tok(values):
    rows = values[0].shape[0]
    stacked = jnp.concatenate([v.reshape(2 * NX, -1) for v in values], axis=0)
    pair = fold(stacked, ((0, 1),))
    whole = fold(pair, ((1, 0), (3, 0), (2, 0)))
    return [whole[n * 2 * NX : (n + 1) * 2 * NX].reshape(rows) for n in range(len(values))]


def swap_z(value, distance):
    def at(y, z, c):
        return y * NZ * NC + z * NC + c

    route = [
        (at(y, z, c), at(y, z ^ distance, c))
        for y in range(NY)
        for z in range(NZ)
        for c in range(NC)
    ]
    return lax.ppermute(value, "group", route)


def spread_cache(cache_keys, cache_values, root, after):
    me = lax.axis_index("group")
    moves = (
        (0, lambda v: group_shift(v, dc=1)),
        (4, lambda v: group_shift(v, dy=1)),
        (1, lambda v: swap_z(v, 1)),
        (2, lambda v: swap_z(v, 2)),
        (3, lambda v: swap_z(v, 4)),
    )
    low, high = cache_keys, cache_values
    for n, (bit, move) in enumerate(moves):
        mine, theirs = (me >> bit) & 1, (root >> bit) & 1
        kept = jnp.where(mine == 1, high, low)
        sent = jnp.where(mine == 1, low, high)
        came = move(sent)
        if n == 1:
            came, _ = lax.optimization_barrier((came, after))
        held = jnp.where(mine == theirs, kept, came)
        half = held.shape[0] // 2
        low, high = held[:half], held[half:]
    for bit, move in moves[::-1]:
        mine = (me >> bit) & 1
        came = move(held)
        if bit:
            low, high = jnp.where(mine == 1, came, held), jnp.where(mine == 1, held, came)
            held = jnp.concatenate([low, high], axis=0)
    return held, came


def attend_kernel(
    heads, scale, order, count, slots, query, ck, cv, ek, ev, nk, nv, *rest
):
    out, keys, values, sems = rest
    span = ck.shape[0]
    tiles = span // TILE

    def copies(parts):
        made = []
        for n, (part, target, row) in enumerate(parts):
            rows = pl.ds(row, part.shape[0])
            made.append(pltpu.make_async_copy(part, target.at[rows], sems.at[n]))
        return made

    fresh = [
        (ek, keys, span),
        (ev, values, span),
        (nk, keys, 2 * span),
        (nv, values, 2 * span),
    ]
    straight = copies([(ck, keys, 0), (cv, values, 0)] + fresh)
    crossed = copies([(cv, keys, 0), (ck, values, 0)] + fresh)

    @pl.when(slots[tiles] == 0)
    def _():
        for copy in straight[:2]:
            copy.start()

    @pl.when(slots[tiles] != 0)
    def _():
        for copy in crossed[:2]:
            copy.start()

    for copy in straight[2:]:
        copy.start()
    for copy in straight:
        copy.wait()

    def all_heads(i, pairs):
        low = lax.broadcasted_iota(jnp.int32, (1, 2 * TILE), 1) < TILE
        for h in range(heads):
            one_tile(h, i, pairs, low)

    def one_tile(h, i, pairs, low):
        from_row = pl.multiple_of(slots[i] * TILE, TILE)
        to_row = pl.multiple_of(i * TILE, TILE)
        cols = pl.ds(h * TILE, TILE)
        at = h * tiles + i
        seen = count[at]
        q = query[pl.ds(from_row, TILE), cols]
        scores, vals = [], []
        for p in range(pairs):
            rows = [
                pl.ds(pl.multiple_of(order[at * MOST + 2 * p + s] * TILE, TILE), TILE)
                for s in range(2)
            ]
            k_pair = jnp.concatenate([keys[r, cols] for r in rows], axis=0)
            vals.append(jnp.concatenate([values[r, cols] for r in rows], axis=0))
            s = lax.dot_general(
                q, k_pair, (((1,), (1,)), ((), ())), preferred_element_type=jnp.float32
            )
            bias = jnp.where(
                low,
                jnp.where(2 * p < seen, 0.0, FAR),
                jnp.where(2 * p + 1 < seen, 0.0, FAR),
            )
            scores.append(s * scale + bias)
        top = scores[0]
        for s in scores[1:]:
            top = jnp.maximum(top, s)
        peak = jnp.max(top, axis=1, keepdims=True)
        total, summed = None, None
        for s, v in zip(scores, vals):
            probs = jnp.exp(s - peak)
            total = probs if total is None else total + probs
            added = jnp.dot(probs.astype(jnp.bfloat16), v, preferred_element_type=jnp.float32)
            summed = added if summed is None else summed + added
        denominator = jnp.sum(total, axis=1, keepdims=True)
        out[pl.ds(to_row, TILE), cols] = (summed / denominator).astype(jnp.bfloat16)

    @pl.loop(0, tiles)
    def _(i):
        all_heads(i, MOST // 2)


def attend(query, parts, order, count, slots, heads):
    rows, width = query.shape
    anywhere = pl.BlockSpec(memory_space=pl.ANY)
    whole = pl.BlockSpec(memory_space=pltpu.VMEM)
    return pl.pallas_call(
        functools.partial(attend_kernel, heads, 1.0 / math.sqrt(width // heads)),
        grid_spec=pltpu.PrefetchScalarGridSpec(
            num_scalar_prefetch=3,
            grid=(),
            in_specs=[whole] + [anywhere] * len(parts),
            out_specs=whole,
            scratch_shapes=[
                pltpu.VMEM((3 * rows, width), jnp.bfloat16),
                pltpu.VMEM((3 * rows, width), jnp.bfloat16),
                pltpu.SemaphoreType.DMA((len(parts),)),
            ],
        ),
        out_shape=jax.ShapeDtypeStruct((rows, width), jnp.bfloat16),
        cost_estimate=pl.CostEstimate(
            flops=4 * rows * width * MOST * TILE,
            transcendentals=rows * heads * MOST * TILE,
            bytes_accessed=16 * rows * width,
        ),
        interpret=INTERPRET,
        name="attend",
    )(order, count, slots, query, *parts)


def tile_lists(tile_mask, is_first, tok):
    tiles, key_tiles = tile_mask.shape[1], tile_mask.shape[2]
    ids = jnp.arange(key_tiles, dtype=jnp.int32)
    earlier = (ids >= tiles) & (ids < 2 * tiles)
    allowed = jnp.where(earlier[None, None, :] & is_first, 0, tile_mask)
    count = jnp.sum(allowed, axis=-1)
    upto = (ids[None, :] <= ids[:, None]).astype(jnp.int32)
    rank = jnp.sum(allowed[:, :, None, :] * upto, axis=-1)
    places = jnp.arange(tiles, dtype=jnp.int32)
    step = (((places >> 1) - (tok >> 1)) & (NX - 1)) * 2 + ((places ^ tok) & 1)
    slots = sum(jnp.where(step == n, slot, 0) for n, slot in enumerate(SLOT_OF))
    physical = jnp.concatenate([places, tiles + slots, 2 * tiles + slots])
    turn = jnp.arange(1, MOST + 1, dtype=jnp.int32)
    picked = (rank[:, :, None, :] == turn[None, None, :, None]) & (allowed[:, :, None, :] > 0)
    order = jnp.sum(jnp.where(picked, physical, 0), axis=-1)
    core = jnp.reshape(lax.axis_index("group") & 1, (1,))
    return order.reshape(-1), count.reshape(-1), jnp.concatenate([slots, core])


def local(
    latents,
    timesteps,
    mod_shift,
    mod_scale,
    w_query,
    w_key,
    w_value,
    query_gain,
    key_gain,
    cache_keys,
    cache_values,
    owners,
    tile_mask,
):
    head_cols = w_query.shape[1]
    width = head_cols * lax.axis_size("tok")
    heads = tile_mask.shape[0]
    root = owners[owners.shape[0] - 1]
    modulated = modulate(latents, timesteps[0], mod_shift, mod_scale)
    own_w = lax.optimization_barrier(jnp.concatenate([w_query, w_key, w_value], axis=1))
    beside_w = group_shift(own_w, dy=1)
    planes = [[y * NZ * NC + n for n in range(NZ * NC)] for y in range(NY)]
    weights = []
    for w in (own_w, beside_w):
        weights.append(
            lax.all_gather(w, "group", axis_index_groups=planes, axis=0, tiled=True)
        )
    depth = weights[0].shape[0]
    modulated = modulate(latents, timesteps[0], mod_shift, mod_scale)
    swapped = jnp.concatenate([modulated[:, depth:], modulated[:, :depth]], axis=1)
    modulated = jnp.where(lax.axis_index("group") < NZ * NC, modulated, swapped)
    blocks = gather_tokens(modulated)
    tokens = jnp.concatenate(blocks, axis=0)

    def projected(first, last):
        parts = []
        for n, w in enumerate(weights):
            parts.append(
                jnp.dot(
                    tokens[:, n * depth : (n + 1) * depth],
                    w[:, first:last],
                    preferred_element_type=jnp.float32,
                )
            )
        return parts[0] + parts[1]

    held, crossed = spread_cache(cache_keys, cache_values, root, blocks[1])
    order, count, slots = tile_lists(
        tile_mask, lax.axis_index("group") == 0, lax.axis_index("tok")
    )
    both = lax.optimization_barrier(projected(0, 2 * head_cols))
    raw_query, raw_key = both[:, :head_cols], both[:, head_cols:]
    query_squares, key_squares = sum_over_tok(
        [jnp.sum(raw_query * raw_query, axis=1), jnp.sum(raw_key * raw_key, axis=1)]
    )
    value_rows = projected(2 * head_cols, 3 * head_cols).astype(jnp.bfloat16)
    earlier_values = from_behind(value_rows, "group", 1)
    key_rows = scaled_rows(raw_key, key_squares, width, key_gain)
    earlier_keys = from_behind(key_rows, "group", 1)
    query_rows = scaled_rows(raw_query, query_squares, width, query_gain)
    parts = (held, crossed, earlier_keys, earlier_values, key_rows, value_rows)
    return attend(query_rows, parts, order, count, slots, heads)


def solution(mesh):
    return jax.shard_map(
        local,
        mesh=mesh,
        in_specs=(
            P(("group", "tok"), None),
            P("group"),
            P(),
            P(),
            P("group", "tok"),
            P("group", "tok"),
            P("group", "tok"),
            P("tok"),
            P("tok"),
            P("group", "tok"),
            P("group", "tok"),
            P(),
            P("tok", None, None),
        ),
        out_specs=P("group", "tok"),
        check_vma=False,
    )
```
